32 devices in a mesh: groups: 2 (over y), row: 16 (over z, x, core).
Axes of the slice: x: 2, y: 2, z: 4, core: 2. Of those that a mesh axis runs over, the one named last changes fastest.
Arguments:
- hidden: bfloat16 [4096, 5120], P(('groups', 'row')), parts along dimension 0, may hold values from -6 to 6
- kv_gain: float32 [5120], replicated, may hold values from 0.5 to 1.5
- kv_weight: bfloat16 [5120, 2048], P('row'), may hold values from -0.25 to 0.25
- query_states: bfloat16 [5120, 256], P('row', 'groups'), parts along dimension 1, may hold values from -6 to 6
- query_gain: float32 [2, 5120], replicated, may hold values from 0.5 to 1.5
- query_weight: bfloat16 [2, 16, 2560, 640], P(None, 'row'), may hold values from -0.078125 to 0.078125
- output_weight: bfloat16 [2, 16, 2560, 640], P(None, 'row'), may hold values from -0.078125 to 0.078125
- block_bounds: int32 [4, 2], P('groups'), parts along dimension 0, may hold values from 0 to 1984, as said below
Outputs:
- mixed: bfloat16 [5120, 256], P('row', 'groups'), parts along dimension 1
The draws below stay inside these ranges and needn't reach their ends.
There are 2 independent parts, one for each index of `groups`. The reference program is written for one: setup_inputs(seed, part) draws one part's arguments, and reference() takes and returns one part's arrays. A program takes and returns all parts, laid end to end along the dimension named above; an argument that names none is the same for every part. Nothing has to cross between parts.
Inputs may be any that keep to these rules, and one draw needn't show every extreme that they name: `block_bounds`: row b is (lowest visible key position, first query position) of query block b; the first is at most the second, and block 0 starts 64 positions before the end of the prefix.
All inputs are finite; a program needn't handle non-finite values.
Results may differ from the reference program's by a relative error of at most 0.035.
Values may be sent and summed in bfloat16 or wider, within the bound.
A program may use at most 128 MiB of HBM per device.

```python
import jax
import jax.numpy as jnp
from jax import lax

D = 5120
HEADS = 40
KVH = 8
HD = 128
QPK = 5
QBLK = 64
NQB = 2
SECTIONS = 2
TOKENS = 2048
TILES = 2
QROWS = 128


def draw_block_bounds(key, part):
    key_one, key_two = jax.random.split(jax.random.fold_in(key, 11), 2)
    last_start = TOKENS - QBLK
    other_start = jax.random.randint(key_one, (NQB - 1,), 0, last_start + 1).astype(jnp.int32)
    starts = jnp.concatenate([jnp.full((1,), last_start, jnp.int32), other_start])
    floors = jax.random.randint(key_two, (NQB,), 0, starts + 1).astype(jnp.int32)
    return jnp.stack([floors, starts], axis=1).astype(jnp.int32)


def steps_of(rng, dims, cuts, least, high):
    level, own = 1.0, jax.random.fold_in(rng, 6)
    for position, shards_of in cuts:
        heights = jnp.exp(jax.random.uniform(jax.random.fold_in(own, position), (shards_of,), jnp.float32, least / len(cuts), high / len(cuts)))
        level = level * jnp.repeat(heights, dims[position] // shards_of).reshape([-1 if axis == position else 1 for axis in range(len(dims))])
    return level


def bell_draw(rng, extent, scale, limit, cuts=(), held_as=jnp.bfloat16):
    values = scale * jax.random.normal(rng, extent, jnp.float32)
    if cuts:
        values = values * steps_of(rng, extent, cuts, -0.22, 0.18)
    return jnp.clip(values, -limit, limit).astype(held_as)


def setup_inputs(seed: int = 0, part: int = 0) -> dict:
    arg_keys = jax.random.split(jax.random.key(seed), 9)
    part_keys = jax.random.split(jax.random.fold_in(arg_keys[8], part), 9)
    return {
        "hidden": bell_draw(part_keys[0], (TOKENS, D), 1.0, 6.0, ((0, 16),)),
        "kv_gain": jnp.clip(1.0 + 0.1 * jax.random.normal(arg_keys[1], (D,), jnp.float32), 0.5, 1.5),
        "kv_weight": bell_draw(arg_keys[2], (D, 2 * KVH * HD), (D // 9) ** -0.5, 0.25, ((0, 16),)),
        "query_states": bell_draw(part_keys[3], (D, QROWS), 1.0, 6.0, ((0, 16),)),
        "query_gain": jnp.clip(1.0 + 0.1 * jax.random.normal(arg_keys[4], (SECTIONS, D), jnp.float32), 0.5, 1.5),
        "query_weight": bell_draw(arg_keys[5], (SECTIONS, KVH * TILES, D // TILES, QPK * HD), D ** -0.5, 0.078125, ((1, 16),)),
        "output_weight": bell_draw(arg_keys[6], (SECTIONS, KVH * TILES, D // TILES, QPK * HD), (HEADS * HD) ** -0.5, 0.078125, ((1, 16),)),
        "block_bounds": draw_block_bounds(jax.random.fold_in(jax.random.fold_in(arg_keys[8], part), 71), part),
    }


CAP = 30.0
EPSILON = 1e-05

def full_weight(blocks):
    arranged = blocks.reshape(TILES, KVH, D // TILES, QPK * HD)
    return jnp.transpose(arranged, (0, 2, 1, 3)).reshape(D, KVH * QPK * HD)

def reference(hidden, kv_gain, kv_weight, query_states, query_gain, query_weight, output_weight, block_bounds):
    hidden_float = hidden.astype(jnp.float32)
    inverse = lax.rsqrt(lax.optimization_barrier(jnp.mean(hidden_float * hidden_float, axis=1, keepdims=True)) + EPSILON)
    normed = (hidden_float * inverse * kv_gain[None, :]).astype(jnp.bfloat16)
    projected = jnp.dot(normed, kv_weight, preferred_element_type=jnp.float32).astype(jnp.bfloat16)
    projected = projected.reshape(TOKENS, KVH, 2, HD)
    key_pos = jnp.arange(TOKENS, dtype=jnp.int32)
    row_number = jnp.arange(QROWS, dtype=jnp.int32)
    query_pos = jnp.repeat(block_bounds[:, 1], QBLK).astype(jnp.int32) + row_number % QBLK
    query_floor = jnp.repeat(block_bounds[:, 0], QBLK).astype(jnp.int32)
    visible = (key_pos[None, :] <= query_pos[:, None]) & (key_pos[None, :] >= query_floor[:, None])
    stream = query_states
    for section in range(SECTIONS):
        stream_float = stream.astype(jnp.float32)
        squares = lax.optimization_barrier(jnp.sum(stream_float * stream_float, axis=0))
        inverse_q = lax.rsqrt(squares / D + EPSILON)
        scaled = (stream_float * query_gain[section][:, None]).astype(jnp.bfloat16)
        w_query = full_weight(query_weight[section])
        queries = lax.dot_general(scaled, w_query, (((0,), (0,)), ((), ())), preferred_element_type=jnp.float32)
        queries = (queries * inverse_q[:, None]).astype(jnp.bfloat16).reshape(QROWS, KVH, QPK, HD)

        def one_group(group):
            q_group = lax.dynamic_index_in_dim(queries, group, 1, keepdims=False).astype(jnp.float32)
            kv_group = lax.dynamic_index_in_dim(projected, group, 1, keepdims=False)
            key_part = kv_group[:, 0, :].astype(jnp.float32)
            value_part = kv_group[:, 1, :].astype(jnp.float32)
            scores = jnp.einsum('qhd,kd->qhk', q_group, key_part) * HD ** (-0.5)
            capped = CAP * jnp.tanh(scores / CAP)
            weights = jnp.where(visible[:, None, :], jnp.exp(capped), 0.0)
            totals = lax.optimization_barrier(jnp.sum(weights, axis=2))
            rounded = lax.optimization_barrier(weights.astype(jnp.bfloat16)).astype(jnp.float32)
            weighted = jnp.einsum('qhk,kd->qhd', rounded, value_part)
            return weighted / totals[:, :, None]
        attended = lax.map(one_group, jnp.arange(KVH, dtype=jnp.int32))
        attended = jnp.transpose(attended, (1, 0, 2, 3)).reshape(QROWS, KVH * QPK * HD).astype(jnp.bfloat16)
        w_out = full_weight(output_weight[section])
        update = lax.dot_general(w_out, attended, (((1,), (1,)), ((), ())), preferred_element_type=jnp.float32)
        stream = (stream_float + update).astype(jnp.bfloat16)
    return stream
```

```python
import functools

import jax
import jax.numpy as jnp
from jax import lax
from jax.experimental import pallas as pl
from jax.experimental.pallas import tpu as pltpu
from jax.sharding import PartitionSpec as P

D = 5120
KVH = 8
HD = 128
QPK = 5
QBLK = 64
NQB = 2
SECTIONS = 2


CAP = 30.0
EPSILON = 1e-05


def swapped(value, axis, distance):
    mask = 2**distance
    pairs = [(source, source ^ mask) for source in range(lax.axis_size(axis))]
    return lax.ppermute(value, axis, pairs)


def halve_sum(first, second, bit_list, split_axis):
    device_index = lax.axis_index("row")
    for bit_number in reversed(bit_list):
        upper_half = device_index // 2**bit_number % 2
        first_low, first_high = jnp.split(first, 2, axis=split_axis)
        second_low, second_high = jnp.split(second, 2, axis=split_axis)
        kept_first = jnp.where(upper_half == 1, first_high, first_low)
        kept_second = jnp.where(upper_half == 1, second_high, second_low)
        sent_first = jnp.where(upper_half == 1, first_low, first_high)
        sent_second = jnp.where(upper_half == 1, second_low, second_high)
        got_first, got_second = (
            swapped(sent_first.astype(jnp.bfloat16), "row", bit_number).astype(sent_first.dtype),
            swapped(sent_second.astype(jnp.bfloat16), "row", bit_number).astype(sent_second.dtype),
        )
        first = kept_first + got_first
        second = kept_second + got_second
    return (first, second)


def halve_one(member, bit_list, split_axis):
    device_index = lax.axis_index("row")
    for bit_number in reversed(bit_list):
        upper_half = device_index // 2**bit_number % 2
        lower_piece, upper_piece = jnp.split(member, 2, axis=split_axis)
        kept = jnp.where(upper_half == 1, upper_piece, lower_piece)
        sent = jnp.where(upper_half == 1, lower_piece, upper_piece)
        member = kept + swapped(sent.astype(jnp.bfloat16), "row", bit_number).astype(sent.dtype)
    return member


def double_gather(gathered, bit_list, join_axis):
    device_index = lax.axis_index("row")
    for bit_number in bit_list:
        upper_half = device_index // 2**bit_number % 2
        partner = swapped(gathered, "row", bit_number)
        gathered = jnp.where(
            upper_half == 1,
            jnp.concatenate([partner, gathered], join_axis),
            jnp.concatenate([gathered, partner], join_axis),
        )
    return gathered


def attend_rows(queries, query_pos, query_floor, key_values, key_pos):
    row_count = queries.shape[0]
    head_width = key_values.shape[1] // 2
    head_count = queries.shape[1] // head_width
    key_part = key_values[:, :head_width]
    value_part = key_values[:, head_width:]
    grouped = queries.reshape(row_count, head_count, head_width)
    scores = jnp.einsum(
        "rhd,kd->rhk", grouped, key_part, preferred_element_type=jnp.float32
    ) * head_width ** (-0.5)
    capped = CAP * jnp.tanh(scores / CAP)
    visible = (key_pos[None, :] <= query_pos[:, None]) & (key_pos[None, :] >= query_floor[:, None])
    weights = jnp.where(visible[:, None, :], jnp.exp(capped), 0.0)
    totals = jnp.sum(weights, axis=2)
    weighted = jnp.einsum(
        "rhk,kd->rhd", weights.astype(jnp.bfloat16), value_part, preferred_element_type=jnp.float32
    )
    return (weighted.reshape(row_count, head_count * head_width), totals)


def on_device(
    hidden, kv_gain, kv_weight, query_states, query_gain, query_weight, output_weight, block_bounds
):
    lane_count = lax.axis_size("row")
    head_bits = KVH.bit_length() - 1
    total_bits = lane_count.bit_length() - 1
    tile_bits = list(range(head_bits))
    group_bits = list(range(head_bits, total_bits))
    tile_count = lane_count // KVH
    device_index = lax.axis_index("row")
    tile_index = device_index // KVH
    token_rows = hidden.shape[0]
    sub_rows = token_rows // tile_count
    pair_width = 2 * HD
    hidden_float = hidden.astype(jnp.float32)
    inverse = lax.rsqrt(jnp.mean(hidden_float * hidden_float, axis=1, keepdims=True) + EPSILON)
    normed = (hidden_float * inverse * kv_gain[None, :]).astype(jnp.bfloat16)
    grouped_rows = normed.reshape(tile_count, sub_rows, D)
    shard_rows = lax.all_gather(kv_weight, "row", axis=0, tiled=True)
    blocked = shard_rows.reshape(shard_rows.shape[0], KVH, pair_width)
    projected = jnp.einsum(
        "psd,dgc->pgsc", grouped_rows, blocked, preferred_element_type=jnp.float32
    )
    outgoing = projected.astype(jnp.bfloat16).reshape(lane_count, sub_rows, pair_width)
    arrived = lax.all_to_all(outgoing, "row", split_axis=0, concat_axis=0, tiled=True)
    key_values = arrived.reshape(lane_count * sub_rows, pair_width)
    source = jnp.arange(lane_count * sub_rows, dtype=jnp.int32)
    key_pos = source // sub_rows * token_rows + tile_index * sub_rows + source % sub_rows
    query_count = NQB * QBLK
    row_number = jnp.arange(query_count, dtype=jnp.int32)
    query_pos = (
        jnp.broadcast_to(block_bounds[:, 1:2], (NQB, QBLK)).reshape(query_count) + row_number % QBLK
    )
    query_floor = jnp.broadcast_to(block_bounds[:, 0:1], (NQB, QBLK)).reshape(query_count)
    rows_share = query_count // tile_count
    slice_depth = D // tile_count
    own_rows = query_states
    stream = double_gather(own_rows, tile_bits, 0)
    for section in range(SECTIONS):
        stream_float = stream.astype(jnp.float32)
        squares = jnp.sum(stream_float * stream_float, axis=0)
        gain_slice = lax.dynamic_slice_in_dim(
            query_gain[section], tile_index * slice_depth, slice_depth
        )
        scaled = (stream_float * gain_slice[:, None]).astype(jnp.bfloat16)
        partial_q = lax.dot_general(
            scaled,
            query_weight[section, 0],
            (((0,), (0,)), ((), ())),
            preferred_element_type=jnp.float32,
        )
        query_sum, square_sum = halve_sum(partial_q, squares, group_bits, 0)
        inverse_q = lax.rsqrt(square_sum / D + EPSILON)
        own_queries = (query_sum * inverse_q[:, None]).astype(jnp.bfloat16)
        all_queries = double_gather(own_queries, group_bits, 0)
        added_all, counted_all = attend_rows(
            all_queries, query_pos, query_floor, key_values, key_pos
        )
        accumulated, totals = halve_sum(added_all, counted_all, group_bits, 0)
        attended = (
            (accumulated.reshape(rows_share, QPK, HD) / totals[:, :, None])
            .reshape(rows_share, QPK * HD)
            .astype(jnp.bfloat16)
        )
        all_attended = double_gather(attended, group_bits, 0)
        update = lax.dot_general(
            output_weight[section, 0],
            all_attended,
            (((1,), (1,)), ((), ())),
            preferred_element_type=jnp.float32,
        )
        own_update = halve_one(update, tile_bits, 0)
        own_rows = (own_rows.astype(jnp.float32) + own_update).astype(jnp.bfloat16)
        if section + 1 < SECTIONS:
            stream = double_gather(own_rows, tile_bits, 0)
    return own_rows


MESH = pl.DeviceIdType.MESH
TILES = 2
CHIPS = KVH // 2
ORDER = (3, 1, 2, 0)
PAIR = 2 * HD
F32 = jnp.float32
BF16 = jnp.bfloat16


def fused_kernel(
    hidden, kv_gain, kv_weight, query_states, query_gain, query_weight, output_weight, bounds,
    out,
    hid, nrm, kvw, xg, wkv, acc, sbuf, rbuf, kvs,
    wq, wo, st, gcol, qsend, qrecv, qh, sqs, sqr,
    oacc, osend, orecv, totb, tsend, trecv, att, us1, ur1, us2, ur2, upd,
    lsem, lw, lx, sx, rx, sf, sw, rw, sk, rk, sst, rst, sq_s, sq_r, so_s, so_r, s1, r1, s2, r2,
):
    tokens, features = hidden.shape
    own = kv_weight.shape[0]
    depth = features // TILES
    chip_rows = 2 * own
    keys = KVH * tokens
    me = lax.axis_index("row")
    tile = me // KVH
    group = me % KVH
    place = group // 2
    core = group % 2
    upper, side = place // 2, place % 2
    other, partner = 1 - tile, 1 - core

    def chip(k):
        a, b = k // 2, k % 2
        return 2 * (upper + a - 2 * a * upper) + (side + b - 2 * b * side)

    def device(in_tile, q, in_core):
        return in_tile * KVH + 2 * q + in_core

    pair = device(tile, place, partner)
    mirror = device(other, place, core)
    mirror_pair = device(other, place, partner)
    pending = []

    def send(src, dst, send_sem, recv_sem, target):
        copy = pltpu.make_async_remote_copy(
            src_ref=src, dst_ref=dst, send_sem=send_sem, recv_sem=recv_sem,
            device_id={"row": target}, device_id_type=MESH,
        )
        copy.start()
        pending.append(copy)

    def arrived(dst, send_sem, recv_sem):
        pltpu.make_async_remote_copy(
            src_ref=dst, dst_ref=dst, send_sem=send_sem, recv_sem=recv_sem,
            device_id={"row": pair}, device_id_type=MESH,
        ).wait_recv()

    load_states = pltpu.make_async_copy(query_states, st.at[0, group], lsem.at[0])
    load_kvw = pltpu.make_async_copy(kv_weight, kvw, lsem.at[1])
    load_hidden = pltpu.make_async_copy(hidden, hid, lsem.at[2])
    load_wq = pltpu.make_async_copy(query_weight, wq, lsem.at[3])
    load_wo = pltpu.make_async_copy(output_weight, wo, lsem.at[4])
    for load in (load_states, load_kvw, load_hidden, load_wq, load_wo):
        load.start()

    barrier = pltpu.get_barrier_semaphore()
    peers = [device(tile, chip(k), cc) for k in (1, 2, 3) for cc in (core, partner)]
    peers += [pair, mirror, mirror_pair]
    for peer in peers:
        pl.semaphore_signal(barrier, inc=1, device_id={"row": peer}, device_id_type=MESH)
    pl.semaphore_wait(barrier, len(peers))

    def stream_sends(s):
        for k in ORDER:
            target = pair if k == 0 else device(tile, chip(k), core)
            send(st.at[s, group], st.at[s, group], sst.at[s, k], rst.at[s, group], target)

    def stream_relay(s):
        for k in (1, 2, 3):
            source = 2 * chip(k) + core
            arrived(st.at[s, source], sst.at[s, k], rst.at[s, source])
            send(st.at[s, source], st.at[s, source], sst.at[s, 4 + k], rst.at[s, source], pair)
        for k in range(CHIPS):
            source = 2 * chip(k) + partner
            arrived(st.at[s, source], sst.at[s, k], rst.at[s, source])

    load_states.wait()
    stream_sends(0)

    load_kvw.wait()
    local = []
    for k in ORDER:
        q = chip(k)
        mine = kvw.at[:, pl.ds(pl.multiple_of((2 * q + core) * PAIR, PAIR), PAIR)]
        theirs = kvw.at[:, pl.ds(pl.multiple_of((2 * q + partner) * PAIR, PAIR), PAIR)]
        send(mine, wkv.at[1, k, core], sw.at[0, k], rw.at[1, k, core], mirror)
        send(theirs, wkv.at[1, k, core], sw.at[1, k], rw.at[1, k, core], mirror_pair)
        send(theirs, wkv.at[0, k, core], sw.at[2, k], rw.at[0, k, core], pair)
        copy = pltpu.make_async_copy(mine, wkv.at[0, k, core], lw.at[k])
        copy.start()
        local.append(copy)

    load_hidden.wait()
    step_rows = 32

    def normalise(i, carry):
        rows = pl.ds(pl.multiple_of(i * step_rows, step_rows), step_rows)
        value = hid[rows, :].astype(F32)
        inverse = lax.rsqrt(jnp.mean(value * value, axis=1, keepdims=True) + EPSILON)
        nrm[rows, :] = (value * inverse * kv_gain[...]).astype(BF16)
        return carry

    lax.fori_loop(0, tokens // step_rows, normalise, 0)

    def feature_block(r, q):
        start = (tile if r == 0 else other) * depth + q * chip_rows
        return nrm.at[:, pl.ds(pl.multiple_of(start, 128), chip_rows)]

    for r in (0, 1):
        for k in ORDER:
            target = pair if k == 0 else device(tile, chip(k), core)
            send(feature_block(r, chip(k)), xg.at[r, group], sx.at[r, k], rx.at[r, group], target)
        copy = pltpu.make_async_copy(feature_block(r, place), xg.at[r, group], lx.at[r])
        copy.start()
        local.append(copy)

    for s in range(SECTIONS):
        def turn(i, carry, s=s):
            cols = pl.ds(pl.multiple_of(tile * depth + i * 128, 128), 128)
            row = query_gain[s : s + 1, cols]
            gcol[s, pl.ds(pl.multiple_of(i * 128, 128), 128), :] = jnp.broadcast_to(row, (128, 128)).T
            return carry

        lax.fori_loop(0, depth // 128, turn, 0)

    def query_partial(s):
        total = jnp.zeros((NQB * QBLK, QPK * HD), F32)
        squares = jnp.zeros((1, NQB * QBLK), F32)
        for j in range(KVH):
            value = st[s, j].astype(F32)
            squares = squares + jnp.sum(value * value, axis=0, keepdims=True)
            scaled = (value * gcol[s, j * own : (j + 1) * own, :]).astype(BF16)
            total = total + lax.dot_general(
                scaled, wq[s, j], (((0,), (0,)), ((), ())), preferred_element_type=F32
            )
        for h in range(QPK):
            part = total[:, h * HD : (h + 1) * HD]
            qh[h] = part
            qsend[s, h] = part.astype(BF16)
        sqs[s] = jnp.broadcast_to(squares, sqs.shape[1:])
        send(qsend.at[s], qrecv.at[s], sq_s.at[s, 0], sq_r.at[s, 0], mirror)
        send(sqs.at[s], sqr.at[s], sq_s.at[s, 1], sq_r.at[s, 1], mirror)

    def query_finish(s):
        arrived(qrecv.at[s], sq_s.at[s, 0], sq_r.at[s, 0])
        arrived(sqr.at[s], sq_s.at[s, 1], sq_r.at[s, 1])
        squares = sqs[s] + sqr[s]
        inverse = lax.rsqrt(squares[0:1, :] / features + EPSILON)
        column = jnp.broadcast_to(inverse, (NQB * QBLK, NQB * QBLK)).T
        for h in range(QPK):
            qfin[h] = ((qh[h] + qrecv[s, h].astype(F32)) * column).astype(BF16)

    qfin = osend.at[SECTIONS]

    stream_relay(0)
    load_wq.wait()
    query_partial(0)

    for r in (0, 1):
        for k in (1, 2, 3):
            source = 2 * chip(k) + core
            arrived(xg.at[r, source], sx.at[r, k], rx.at[r, source])
            send(xg.at[r, source], xg.at[r, source], sf.at[r, k], rx.at[r, source], pair)

    row_step = 256
    sources = row_step // tokens

    def product(r, k, i):
        left = xg[r, pl.ds(i * sources, sources)].reshape(row_step, chip_rows)
        right = wkv[r, k].reshape(chip_rows, PAIR)
        return jnp.dot(left, right, preferred_element_type=F32)

    def take(r):
        for k in range(CHIPS):
            source = 2 * chip(k) + partner
            arrived(xg.at[r, source], sx.at[r, k], rx.at[r, source])

    for copy in local:
        copy.wait()
    take(0)
    for k in ORDER:
        arrived(wkv.at[0, k, partner], sw.at[2, k], rw.at[0, k, partner])

        def first(i, carry, k=k):
            acc[k, pl.ds(pl.multiple_of(i * row_step, row_step), row_step), :] = product(0, k, i)
            return carry

        lax.fori_loop(0, keys // row_step, first, 0)
    take(1)
    for k in ORDER:
        arrived(wkv.at[1, k, 0], sw.at[0, k], rw.at[1, k, 0])
        arrived(wkv.at[1, k, 1], sw.at[1, k], rw.at[1, k, 1])

        def second(i, carry, k=k):
            rows = pl.ds(pl.multiple_of(i * row_step, row_step), row_step)
            value = acc[k, rows, :] + product(1, k, i)
            if k == 0:
                acc[k, rows, :] = value
            else:
                sbuf[k, rows, :] = value.astype(BF16)
            return carry

        lax.fori_loop(0, keys // row_step, second, 0)
        if k:
            send(sbuf.at[k], rbuf.at[k], sk.at[k], rk.at[k], device(tile, chip(k), core))
    for k in (1, 2, 3):
        arrived(rbuf.at[k], sk.at[k], rk.at[k])

    def join(i, carry):
        rows = pl.ds(pl.multiple_of(i * row_step, row_step), row_step)
        value = acc[0, rows, :]
        for k in (1, 2, 3):
            value = value + rbuf[k, rows, :].astype(F32)
        kvs[rows, :] = value.astype(BF16)
        return carry

    lax.fori_loop(0, keys // row_step, join, 0)

    load_wo.wait()
    rows_of = NQB * QBLK
    for s in range(SECTIONS):
        query_finish(s)

        def attend(i, carry):
            h, b = i // NQB, i % NQB
            rows = pl.ds(pl.multiple_of(b * QBLK, QBLK), QBLK)
            score = lax.dot_general(
                qfin[h, rows, :], kvs[:, :HD], (((1,), (1,)), ((), ())), preferred_element_type=F32
            ) * HD ** (-0.5)
            capped = CAP * jnp.tanh(score / CAP)
            position = tile * keys + lax.broadcasted_iota(jnp.int32, (QBLK, keys), 1)
            last = bounds[b, 1] + lax.broadcasted_iota(jnp.int32, (QBLK, keys), 0)
            visible = (position <= last) & (position >= bounds[b, 0])
            weight = jnp.where(visible, jnp.exp(capped), 0.0)
            totb[h, rows, :] = jnp.broadcast_to(jnp.sum(weight, axis=1, keepdims=True), (QBLK, HD))
            oacc[h, rows, :] = jnp.dot(weight.astype(BF16), kvs[:, HD:], preferred_element_type=F32)
            return carry

        lax.fori_loop(0, QPK * NQB, attend, 0)
        lane = lax.broadcasted_iota(jnp.int32, (rows_of, HD), 1)
        table = jnp.zeros((rows_of, HD), F32)
        for h in range(QPK):
            osend[s, h] = oacc[h].astype(BF16)
            table = jnp.where(lane == h, totb[h], table)
        tsend[s] = table.T[0:8, :]
        send(osend.at[s], orecv.at[s], so_s.at[s, 0], so_r.at[s, 0], mirror)
        send(tsend.at[s], trecv.at[s], so_s.at[s, 1], so_r.at[s, 1], mirror)
        arrived(trecv.at[s], so_s.at[s, 1], so_r.at[s, 1])
        arrived(orecv.at[s], so_s.at[s, 0], so_r.at[s, 0])
        table = jnp.concatenate([trecv[s], jnp.zeros((HD - 8, rows_of), F32)], axis=0).T
        for h in range(QPK):
            total = totb[h] + table[:, h : h + 1]
            value = (oacc[h] + orecv[s, h].astype(F32)) / total
            att[:, h * HD : (h + 1) * HD] = value.astype(BF16)

        def update(j):
            return lax.dot_general(
                wo[s, j], att[...], (((1,), (1,)), ((), ())), preferred_element_type=F32
            )

        for k in ORDER:
            us1[s, k] = update(2 * chip(k) + partner).astype(BF16)
            send(us1.at[s, k], ur1.at[s, k], s1.at[s, k], r1.at[s, k], pair)
        for k in ORDER:
            value = update(2 * chip(k) + core)
            arrived(ur1.at[s, k], s1.at[s, k], r1.at[s, k])
            value = value + ur1[s, k].astype(F32)
            if k:
                us2[s, k] = value.astype(BF16)
                send(us2.at[s, k], ur2.at[s, k], s2.at[s, k], r2.at[s, k], device(tile, chip(k), core))
            else:
                upd[...] = value + st[s, group].astype(F32)
        for k in (1, 2, 3):
            arrived(ur2.at[s, k], s2.at[s, k], r2.at[s, k])
        value = upd[...]
        for k in (1, 2, 3):
            value = value + ur2[s, k].astype(F32)
        if s + 1 < SECTIONS:
            st[s + 1, group] = value.astype(BF16)
            stream_sends(s + 1)
            stream_relay(s + 1)
            query_partial(s + 1)
        else:
            out[...] = value.astype(BF16)
    for copy in pending:
        copy.wait_send()


def on_kernel(
    hidden, kv_gain, kv_weight, query_states, query_gain, query_weight, output_weight, block_bounds
):
    tokens, features = hidden.shape
    own = kv_weight.shape[0]
    depth = features // TILES
    chip_rows = 2 * own
    keys = KVH * tokens
    rows = NQB * QBLK
    vmem, dma = pltpu.VMEM, pltpu.SemaphoreType.DMA
    scratch = [
        vmem((tokens, features), BF16),
        vmem((tokens, features), BF16),
        vmem(kv_weight.shape, BF16),
        vmem((TILES, KVH, tokens, chip_rows), BF16),
        vmem((TILES, CHIPS, 2, own, PAIR), BF16),
        vmem((CHIPS, keys, PAIR), F32),
        vmem((CHIPS, keys, PAIR), BF16),
        vmem((CHIPS, keys, PAIR), BF16),
        vmem((keys, PAIR), BF16),
        vmem((SECTIONS, KVH, own, QPK * HD), BF16),
        vmem((SECTIONS, KVH, own, QPK * HD), BF16),
        vmem((SECTIONS, KVH, own, rows), BF16),
        vmem((SECTIONS, depth, rows), F32),
        vmem((SECTIONS, QPK, rows, HD), BF16),
        vmem((SECTIONS, QPK, rows, HD), BF16),
        vmem((QPK, rows, HD), F32),
        vmem((SECTIONS, 8, rows), F32),
        vmem((SECTIONS, 8, rows), F32),
        vmem((QPK, rows, HD), F32),
        vmem((SECTIONS + 1, QPK, rows, HD), BF16),
        vmem((SECTIONS, QPK, rows, HD), BF16),
        vmem((QPK, rows, HD), F32),
        vmem((SECTIONS, 8, rows), F32),
        vmem((SECTIONS, 8, rows), F32),
        vmem((rows, QPK * HD), BF16),
        vmem((SECTIONS, CHIPS, own, rows), BF16),
        vmem((SECTIONS, CHIPS, own, rows), BF16),
        vmem((SECTIONS, CHIPS, own, rows), BF16),
        vmem((SECTIONS, CHIPS, own, rows), BF16),
        vmem((own, rows), F32),
        dma((5,)), dma((4,)), dma((2,)), dma((2, 4)), dma((2, 8)), dma((2, 4)),
        dma((3, 4)), dma((2, 4, 2)), dma((4,)), dma((4,)),
        dma((SECTIONS, 8)), dma((SECTIONS, 8)),
        dma((SECTIONS, 2)), dma((SECTIONS, 2)), dma((SECTIONS, 2)), dma((SECTIONS, 2)),
        dma((SECTIONS, 4)), dma((SECTIONS, 4)), dma((SECTIONS, 4)), dma((SECTIONS, 4)),
    ]
    anywhere = pl.BlockSpec(memory_space=pl.ANY)
    whole = pl.BlockSpec(memory_space=pltpu.VMEM)
    return pl.pallas_call(
        fused_kernel,
        out_shape=jax.ShapeDtypeStruct(query_states.shape, BF16),
        in_specs=[
            anywhere, whole, anywhere, anywhere, whole, anywhere, anywhere,
            pl.BlockSpec(memory_space=pltpu.SMEM),
        ],
        out_specs=whole,
        scratch_shapes=scratch,
        compiler_params=pltpu.CompilerParams(
            collective_id=0, has_side_effects=True, vmem_limit_bytes=60 * 2**20
        ),
    )(
        hidden,
        kv_gain[None, :],
        kv_weight,
        query_states,
        query_gain,
        query_weight.reshape(SECTIONS, KVH, own, QPK * HD),
        output_weight.reshape(SECTIONS, KVH, own, QPK * HD),
        block_bounds,
    )


def choose(*args):
    tiles = lax.axis_size("row") // KVH
    if tiles == TILES and 2 * args[2].shape[0] % 128 == 0:
        return on_kernel(*args)
    return on_device(*args)


def solution(mesh):
    in_specs = (
        P(("groups", "row"), None),
        P(),
        P("row", None),
        P("row", "groups"),
        P(),
        P(None, "row", None, None),
        P(None, "row", None, None),
        P("groups", None),
    )
    out_specs = P("row", "groups")
    return jax.shard_map(
        choose, mesh=mesh, in_specs=in_specs, out_specs=out_specs, check_vma=False
    )
```

```python
import functools

import jax
import jax.numpy as jnp
from jax import lax
from jax.experimental import pallas as pl
from jax.experimental.pallas import tpu as pltpu
from jax.sharding import PartitionSpec as P

D = 5120
KVH = 8
HD = 128
QPK = 5
QBLK = 64
NQB = 2
SECTIONS = 2


CAP = 30.0
EPSILON = 1e-05


def swapped(value, axis, distance):
    mask = 2**distance
    pairs = [(source, source ^ mask) for source in range(lax.axis_size(axis))]
    return lax.ppermute(value, axis, pairs)


def halve_sum(first, second, bit_list, split_axis):
    device_index = lax.axis_index("row")
    for bit_number in reversed(bit_list):
        upper_half = device_index // 2**bit_number % 2
        first_low, first_high = jnp.split(first, 2, axis=split_axis)
        second_low, second_high = jnp.split(second, 2, axis=split_axis)
        kept_first = jnp.where(upper_half == 1, first_high, first_low)
        kept_second = jnp.where(upper_half == 1, second_high, second_low)
        sent_first = jnp.where(upper_half == 1, first_low, first_high)
        sent_second = jnp.where(upper_half == 1, second_low, second_high)
        got_first, got_second = (
            swapped(sent_first.astype(jnp.bfloat16), "row", bit_number).astype(sent_first.dtype),
            swapped(sent_second.astype(jnp.bfloat16), "row", bit_number).astype(sent_second.dtype),
        )
        first = kept_first + got_first
        second = kept_second + got_second
    return (first, second)


def halve_one(member, bit_list, split_axis):
    device_index = lax.axis_index("row")
    for bit_number in reversed(bit_list):
        upper_half = device_index // 2**bit_number % 2
        lower_piece, upper_piece = jnp.split(member, 2, axis=split_axis)
        kept = jnp.where(upper_half == 1, upper_piece, lower_piece)
        sent = jnp.where(upper_half == 1, lower_piece, upper_piece)
        member = kept + swapped(sent.astype(jnp.bfloat16), "row", bit_number).astype(sent.dtype)
    return member


def double_gather(gathered, bit_list, join_axis):
    device_index = lax.axis_index("row")
    for bit_number in bit_list:
        upper_half = device_index // 2**bit_number % 2
        partner = swapped(gathered, "row", bit_number)
        gathered = jnp.where(
            upper_half == 1,
            jnp.concatenate([partner, gathered], join_axis),
            jnp.concatenate([gathered, partner], join_axis),
        )
    return gathered


def attend_rows(queries, query_pos, query_floor, key_values, key_pos):
    row_count = queries.shape[0]
    head_width = key_values.shape[1] // 2
    head_count = queries.shape[1] // head_width
    key_part = key_values[:, :head_width]
    value_part = key_values[:, head_width:]
    grouped = queries.reshape(row_count, head_count, head_width)
    scores = jnp.einsum(
        "rhd,kd->rhk", grouped, key_part, preferred_element_type=jnp.float32
    ) * head_width ** (-0.5)
    capped = CAP * jnp.tanh(scores / CAP)
    visible = (key_pos[None, :] <= query_pos[:, None]) & (key_pos[None, :] >= query_floor[:, None])
    weights = jnp.where(visible[:, None, :], jnp.exp(capped), 0.0)
    totals = jnp.sum(weights, axis=2)
    weighted = jnp.einsum(
        "rhk,kd->rhd", weights.astype(jnp.bfloat16), value_part, preferred_element_type=jnp.float32
    )
    return (weighted.reshape(row_count, head_count * head_width), totals)


def on_device(
    hidden, kv_gain, kv_weight, query_states, query_gain, query_weight, output_weight, block_bounds
):
    lane_count = lax.axis_size("row")
    head_bits = KVH.bit_length() - 1
    total_bits = lane_count.bit_length() - 1
    tile_bits = list(range(head_bits))
    group_bits = list(range(head_bits, total_bits))
    tile_count = lane_count // KVH
    device_index = lax.axis_index("row")
    tile_index = device_index // KVH
    token_rows = hidden.shape[0]
    sub_rows = token_rows // tile_count
    pair_width = 2 * HD
    hidden_float = hidden.astype(jnp.float32)
    inverse = lax.rsqrt(jnp.mean(hidden_float * hidden_float, axis=1, keepdims=True) + EPSILON)
    normed = (hidden_float * inverse * kv_gain[None, :]).astype(jnp.bfloat16)
    grouped_rows = normed.reshape(tile_count, sub_rows, D)
    shard_rows = lax.all_gather(kv_weight, "row", axis=0, tiled=True)
    blocked = shard_rows.reshape(shard_rows.shape[0], KVH, pair_width)
    projected = jnp.einsum(
        "psd,dgc->pgsc", grouped_rows, blocked, preferred_element_type=jnp.float32
    )
    outgoing = projected.astype(jnp.bfloat16).reshape(lane_count, sub_rows, pair_width)
    arrived = lax.all_to_all(outgoing, "row", split_axis=0, concat_axis=0, tiled=True)
    key_values = arrived.reshape(lane_count * sub_rows, pair_width)
    source = jnp.arange(lane_count * sub_rows, dtype=jnp.int32)
    key_pos = source // sub_rows * token_rows + tile_index * sub_rows + source % sub_rows
    query_count = NQB * QBLK
    row_number = jnp.arange(query_count, dtype=jnp.int32)
    query_pos = (
        jnp.broadcast_to(block_bounds[:, 1:2], (NQB, QBLK)).reshape(query_count) + row_number % QBLK
    )
    query_floor = jnp.broadcast_to(block_bounds[:, 0:1], (NQB, QBLK)).reshape(query_count)
    rows_share = query_count // tile_count
    slice_depth = D // tile_count
    own_rows = query_states
    stream = double_gather(own_rows, tile_bits, 0)
    for section in range(SECTIONS):
        stream_float = stream.astype(jnp.float32)
        squares = jnp.sum(stream_float * stream_float, axis=0)
        gain_slice = lax.dynamic_slice_in_dim(
            query_gain[section], tile_index * slice_depth, slice_depth
        )
        scaled = (stream_float * gain_slice[:, None]).astype(jnp.bfloat16)
        partial_q = lax.dot_general(
            scaled,
            query_weight[section, 0],
            (((0,), (0,)), ((), ())),
            preferred_element_type=jnp.float32,
        )
        query_sum, square_sum = halve_sum(partial_q, squares, group_bits, 0)
        inverse_q = lax.rsqrt(square_sum / D + EPSILON)
        own_queries = (query_sum * inverse_q[:, None]).astype(jnp.bfloat16)
        all_queries = double_gather(own_queries, group_bits, 0)
        added_all, counted_all = attend_rows(
            all_queries, query_pos, query_floor, key_values, key_pos
        )
        accumulated, totals = halve_sum(added_all, counted_all, group_bits, 0)
        attended = (
            (accumulated.reshape(rows_share, QPK, HD) / totals[:, :, None])
            .reshape(rows_share, QPK * HD)
            .astype(jnp.bfloat16)
        )
        all_attended = double_gather(attended, group_bits, 0)
        update = lax.dot_general(
            output_weight[section, 0],
            all_attended,
            (((1,), (1,)), ((), ())),
            preferred_element_type=jnp.float32,
        )
        own_update = halve_one(update, tile_bits, 0)
        own_rows = (own_rows.astype(jnp.float32) + own_update).astype(jnp.bfloat16)
        if section + 1 < SECTIONS:
            stream = double_gather(own_rows, tile_bits, 0)
    return own_rows


MESH = pl.DeviceIdType.MESH
TILES = 2
CHIPS = KVH // 2
ORDER = (3, 2, 1, 0)
PAIR = 2 * HD
F32 = jnp.float32
BF16 = jnp.bfloat16


def fused_kernel(
    hidden, kv_gain, kv_weight, query_states, query_gain, query_weight, output_weight, bounds,
    out,
    hid, nrm, kvw, xg, wkv, acc, sbuf, rbuf, kvs,
    wq, wo, st, gcol, qsend, qrecv, qh, sqs, sqr,
    oacc, osend, orecv, totb, tsend, trecv, att, us1, ur1, us2, ur2, upd,
    lsem, lw, lx, sx, rx, sf, sw, sy, rw, sk, rk, sst, rst, sq_s, sq_r, so_s, so_r, s1, r1, s2, r2,
):
    tokens, features = hidden.shape
    own = kv_weight.shape[0]
    depth = features // TILES
    chip_rows = 2 * own
    keys = KVH * tokens
    me = lax.axis_index("row")
    plane = lax.axis_index("groups")
    tile = me // KVH
    group = me % KVH
    place = group // 2
    core = group % 2
    upper, side = place // 2, place % 2
    other, partner = 1 - tile, 1 - core

    def chip(k):
        a, b = k // 2, k % 2
        return 2 * (upper + a - 2 * a * upper) + (side + b - 2 * b * side)

    def device(in_tile, q, in_core):
        return in_tile * KVH + 2 * q + in_core

    pair = device(tile, place, partner)
    mirror = device(other, place, core)
    mirror_pair = device(other, place, partner)
    pending = []

    def send(src, dst, send_sem, recv_sem, target):
        copy = pltpu.make_async_remote_copy(
            src_ref=src, dst_ref=dst, send_sem=send_sem, recv_sem=recv_sem,
            device_id=target if isinstance(target, dict) else {"row": target},
            device_id_type=MESH,
        )
        copy.start()
        pending.append(copy)

    def arrived(dst, send_sem, recv_sem):
        pltpu.make_async_remote_copy(
            src_ref=dst, dst_ref=dst, send_sem=send_sem, recv_sem=recv_sem,
            device_id={"row": pair}, device_id_type=MESH,
        ).wait_recv()

    load_states = pltpu.make_async_copy(query_states, st.at[0, group], lsem.at[0])
    load_kvw = pltpu.make_async_copy(kv_weight, kvw, lsem.at[1])
    load_hidden = pltpu.make_async_copy(hidden, hid, lsem.at[2])
    load_wq = pltpu.make_async_copy(query_weight, wq, lsem.at[3])
    load_wo = pltpu.make_async_copy(output_weight, wo, lsem.at[4])
    for load in (load_states, load_kvw, load_hidden, load_wq, load_wo):
        load.start()

    barrier = pltpu.get_barrier_semaphore()
    peers = [device(tile, chip(k), cc) for k in (1, 2, 3) for cc in (core, partner)]
    peers += [pair, mirror, mirror_pair]
    for peer in peers:
        pl.semaphore_signal(barrier, inc=1, device_id={"row": peer}, device_id_type=MESH)
    across = {"groups": 1 - plane}
    pl.semaphore_signal(barrier, inc=1, device_id=across, device_id_type=MESH)
    pl.semaphore_wait(barrier, len(peers) + 1)

    def stream_sends(s):
        for k in ORDER:
            target = pair if k == 0 else device(tile, chip(k), core)
            send(st.at[s, group], st.at[s, group], sst.at[s, k], rst.at[s, group], target)

    def stream_relay(s):
        for k in (1, 2, 3):
            source = 2 * chip(k) + core
            arrived(st.at[s, source], sst.at[s, k], rst.at[s, source])
            send(st.at[s, source], st.at[s, source], sst.at[s, 4 + k], rst.at[s, source], pair)
        for k in range(CHIPS):
            source = 2 * chip(k) + partner
            arrived(st.at[s, source], sst.at[s, k], rst.at[s, source])

    load_states.wait()
    stream_sends(0)

    load_kvw.wait()
    local = []

    def head_columns(k, in_core):
        return kvw.at[:, pl.ds(pl.multiple_of((2 * chip(k) + in_core) * PAIR, PAIR), PAIR)]

    def mirror_sends(i):
        k = CHIPS - 1 - (2 * i + plane)
        send(head_columns(k, core), wkv.at[1, k, core], sw.at[0, i], rw.at[1, k, core], mirror)
        send(head_columns(k, partner), wkv.at[1, k, core], sw.at[1, i], rw.at[1, k, core], mirror_pair)

    def mirror_relay(i):
        k = CHIPS - 1 - (2 * i + plane)
        for cc in (0, 1):
            arrived(wkv.at[1, k, cc], sw.at[0, i], rw.at[1, k, cc])
            send(wkv.at[1, k, cc], wkv.at[1, k, cc], sy.at[i, cc], rw.at[1, k, cc], across)

    def mirror_take(i):
        k = CHIPS - 1 - (2 * i + 1 - plane)
        for cc in (0, 1):
            arrived(wkv.at[1, k, cc], sw.at[0, i], rw.at[1, k, cc])

    mirror_sends(0)
    for k in ORDER:
        send(head_columns(k, partner), wkv.at[0, k, core], sw.at[2, k], rw.at[0, k, core], pair)
        copy = pltpu.make_async_copy(head_columns(k, core), wkv.at[0, k, core], lw.at[k])
        copy.start()
        local.append(copy)

    load_hidden.wait()
    step_rows = 32

    def normalise(i, carry):
        rows = pl.ds(pl.multiple_of(i * step_rows, step_rows), step_rows)
        value = hid[rows, :].astype(F32)
        inverse = lax.rsqrt(jnp.mean(value * value, axis=1, keepdims=True) + EPSILON)
        nrm[rows, :] = (value * inverse * kv_gain[...]).astype(BF16)
        return carry

    lax.fori_loop(0, tokens // step_rows, normalise, 0)

    def feature_block(r, q):
        start = (tile if r == 0 else other) * depth + q * chip_rows
        return nrm.at[:, pl.ds(pl.multiple_of(start, 128), chip_rows)]

    for r in (0, 1):
        for k in ORDER:
            target = pair if k == 0 else device(tile, chip(k), core)
            send(feature_block(r, chip(k)), xg.at[r, group], sx.at[r, k], rx.at[r, group], target)
        copy = pltpu.make_async_copy(feature_block(r, place), xg.at[r, group], lx.at[r])
        copy.start()
        local.append(copy)
    mirror_sends(1)

    for s in range(SECTIONS):
        def turn(i, carry, s=s):
            cols = pl.ds(pl.multiple_of(tile * depth + i * 128, 128), 128)
            row = query_gain[s : s + 1, cols]
            gcol[s, pl.ds(pl.multiple_of(i * 128, 128), 128), :] = jnp.broadcast_to(row, (128, 128)).T
            return carry

        lax.fori_loop(0, depth // 128, turn, 0)

    def query_partial(s):
        total = jnp.zeros((NQB * QBLK, QPK * HD), F32)
        squares = jnp.zeros((1, NQB * QBLK), F32)
        for j in range(KVH):
            value = st[s, j].astype(F32)
            squares = squares + jnp.sum(value * value, axis=0, keepdims=True)
            scaled = (value * gcol[s, j * own : (j + 1) * own, :]).astype(BF16)
            total = total + lax.dot_general(
                scaled, wq[s, j], (((0,), (0,)), ((), ())), preferred_element_type=F32
            )
        for h in range(QPK):
            part = total[:, h * HD : (h + 1) * HD]
            qh[h] = part
            qsend[s, h] = part.astype(BF16)
            if h == 0:
                sqs[s] = jnp.broadcast_to(squares, sqs.shape[1:])
                send(sqs.at[s], sqr.at[s], sq_s.at[s, QPK], sq_r.at[s, QPK], mirror)
            send(qsend.at[s, h], qrecv.at[s, h], sq_s.at[s, h], sq_r.at[s, h], mirror)

    def query_finish(s):
        arrived(sqr.at[s], sq_s.at[s, QPK], sq_r.at[s, QPK])
        squares = sqs[s] + sqr[s]
        inverse = lax.rsqrt(squares[0:1, :] / features + EPSILON)
        return jnp.broadcast_to(inverse, (NQB * QBLK, NQB * QBLK)).T

    qfin = osend.at[SECTIONS]

    stream_relay(0)
    load_wq.wait()
    query_partial(0)

    for r in (0, 1):
        for k in (1, 2, 3):
            source = 2 * chip(k) + core
            arrived(xg.at[r, source], sx.at[r, k], rx.at[r, source])
            send(xg.at[r, source], xg.at[r, source], sf.at[r, k], rx.at[r, source], pair)

    row_step = 256
    sources = row_step // tokens

    def product(r, k, i):
        left = xg[r, pl.ds(i * sources, sources)].reshape(row_step, chip_rows)
        right = wkv[r, k].reshape(chip_rows, PAIR)
        return jnp.dot(left, right, preferred_element_type=F32)

    def take(r):
        for k in range(CHIPS):
            source = 2 * chip(k) + partner
            arrived(xg.at[r, source], sx.at[r, k], rx.at[r, source])

    for copy in local:
        copy.wait()
    mirror_relay(0)
    take(0)
    for k in ORDER:
        arrived(wkv.at[0, k, partner], sw.at[2, k], rw.at[0, k, partner])

        def first(i, carry, k=k):
            acc[k, pl.ds(pl.multiple_of(i * row_step, row_step), row_step), :] = product(0, k, i)
            return carry

        lax.fori_loop(0, keys // row_step, first, 0)
    take(1)
    for k in ORDER:
        if k == CHIPS - 1:
            mirror_take(0)
        if k == 1:
            mirror_relay(1)
            mirror_take(1)

        def second(i, carry, k=k):
            rows = pl.ds(pl.multiple_of(i * row_step, row_step), row_step)
            value = acc[k, rows, :] + product(1, k, i)
            if k == 0:
                acc[k, rows, :] = value
            else:
                sbuf[k, rows, :] = value.astype(BF16)
            return carry

        lax.fori_loop(0, keys // row_step, second, 0)
        if k:
            send(sbuf.at[k], rbuf.at[k], sk.at[k], rk.at[k], device(tile, chip(k), core))
    for k in (1, 2, 3):
        arrived(rbuf.at[k], sk.at[k], rk.at[k])

    def join(i, carry):
        rows = pl.ds(pl.multiple_of(i * row_step, row_step), row_step)
        value = acc[0, rows, :]
        for k in (1, 2, 3):
            value = value + rbuf[k, rows, :].astype(F32)
        kvs[rows, :] = value.astype(BF16)
        return carry

    lax.fori_loop(0, keys // row_step, join, 0)

    load_wo.wait()
    rows_of = NQB * QBLK
    for s in range(SECTIONS):
        column = query_finish(s)

        def attend(b, carry, h):
            rows = pl.ds(pl.multiple_of(b * QBLK, QBLK), QBLK)
            score = lax.dot_general(
                qfin[h, rows, :], kvs[:, :HD], (((1,), (1,)), ((), ())), preferred_element_type=F32
            ) * HD ** (-0.5)
            capped = CAP * jnp.tanh(score / CAP)
            position = tile * keys + lax.broadcasted_iota(jnp.int32, (QBLK, keys), 1)
            last = bounds[b, 1] + lax.broadcasted_iota(jnp.int32, (QBLK, keys), 0)
            visible = (position <= last) & (position >= bounds[b, 0])
            weight = jnp.where(visible, jnp.exp(capped), 0.0)
            totb[h, rows, :] = jnp.broadcast_to(jnp.sum(weight, axis=1, keepdims=True), (QBLK, HD))
            oacc[h, rows, :] = jnp.dot(weight.astype(BF16), kvs[:, HD:], preferred_element_type=F32)
            return carry

        for h in range(QPK):
            arrived(qrecv.at[s, h], sq_s.at[s, h], sq_r.at[s, h])
            qfin[h] = ((qh[h] + qrecv[s, h].astype(F32)) * column).astype(BF16)
            lax.fori_loop(0, NQB, functools.partial(attend, h=h), 0)
            osend[s, h] = oacc[h].astype(BF16)
            send(osend.at[s, h], orecv.at[s, h], so_s.at[s, h], so_r.at[s, h], mirror)
        lane = lax.broadcasted_iota(jnp.int32, (rows_of, HD), 1)
        table = jnp.zeros((rows_of, HD), F32)
        for h in range(QPK):
            table = jnp.where(lane == h, totb[h], table)
        tsend[s] = table.T[0:8, :]
        send(tsend.at[s], trecv.at[s], so_s.at[s, QPK], so_r.at[s, QPK], mirror)
        arrived(trecv.at[s], so_s.at[s, QPK], so_r.at[s, QPK])
        table = jnp.concatenate([trecv[s], jnp.zeros((HD - 8, rows_of), F32)], axis=0).T
        for h in range(QPK):
            arrived(orecv.at[s, h], so_s.at[s, h], so_r.at[s, h])
            total = totb[h] + table[:, h : h + 1]
            value = (oacc[h] + orecv[s, h].astype(F32)) / total
            att[:, h * HD : (h + 1) * HD] = value.astype(BF16)

        def update(j):
            return lax.dot_general(
                wo[s, j], att[...], (((1,), (1,)), ((), ())), preferred_element_type=F32
            )

        for k in ORDER:
            us1[s, k] = update(2 * chip(k) + partner).astype(BF16)
            send(us1.at[s, k], ur1.at[s, k], s1.at[s, k], r1.at[s, k], pair)
        for k in ORDER:
            value = update(2 * chip(k) + core)
            arrived(ur1.at[s, k], s1.at[s, k], r1.at[s, k])
            value = value + ur1[s, k].astype(F32)
            if k:
                us2[s, k] = value.astype(BF16)
                send(us2.at[s, k], ur2.at[s, k], s2.at[s, k], r2.at[s, k], device(tile, chip(k), core))
            else:
                upd[...] = value + st[s, group].astype(F32)
        for k in (1, 2, 3):
            arrived(ur2.at[s, k], s2.at[s, k], r2.at[s, k])
        value = upd[...]
        for k in (1, 2, 3):
            value = value + ur2[s, k].astype(F32)
        if s + 1 < SECTIONS:
            st[s + 1, group] = value.astype(BF16)
            stream_sends(s + 1)
            stream_relay(s + 1)
            query_partial(s + 1)
        else:
            out[...] = value.astype(BF16)
    for copy in pending:
        copy.wait_send()


def on_kernel(
    hidden, kv_gain, kv_weight, query_states, query_gain, query_weight, output_weight, block_bounds
):
    tokens, features = hidden.shape
    own = kv_weight.shape[0]
    depth = features // TILES
    chip_rows = 2 * own
    keys = KVH * tokens
    rows = NQB * QBLK
    vmem, dma = pltpu.VMEM, pltpu.SemaphoreType.DMA
    scratch = [
        vmem((tokens, features), BF16),
        vmem((tokens, features), BF16),
        vmem(kv_weight.shape, BF16),
        vmem((TILES, KVH, tokens, chip_rows), BF16),
        vmem((TILES, CHIPS, 2, own, PAIR), BF16),
        vmem((CHIPS, keys, PAIR), F32),
        vmem((CHIPS, keys, PAIR), BF16),
        vmem((CHIPS, keys, PAIR), BF16),
        vmem((keys, PAIR), BF16),
        vmem((SECTIONS, KVH, own, QPK * HD), BF16),
        vmem((SECTIONS, KVH, own, QPK * HD), BF16),
        vmem((SECTIONS, KVH, own, rows), BF16),
        vmem((SECTIONS, depth, rows), F32),
        vmem((SECTIONS, QPK, rows, HD), BF16),
        vmem((SECTIONS, QPK, rows, HD), BF16),
        vmem((QPK, rows, HD), F32),
        vmem((SECTIONS, 8, rows), F32),
        vmem((SECTIONS, 8, rows), F32),
        vmem((QPK, rows, HD), F32),
        vmem((SECTIONS + 1, QPK, rows, HD), BF16),
        vmem((SECTIONS, QPK, rows, HD), BF16),
        vmem((QPK, rows, HD), F32),
        vmem((SECTIONS, 8, rows), F32),
        vmem((SECTIONS, 8, rows), F32),
        vmem((rows, QPK * HD), BF16),
        vmem((SECTIONS, CHIPS, own, rows), BF16),
        vmem((SECTIONS, CHIPS, own, rows), BF16),
        vmem((SECTIONS, CHIPS, own, rows), BF16),
        vmem((SECTIONS, CHIPS, own, rows), BF16),
        vmem((own, rows), F32),
        dma((5,)), dma((4,)), dma((2,)), dma((2, 4)), dma((2, 8)), dma((2, 4)),
        dma((3, 4)), dma((2, 2)), dma((2, 4, 2)), dma((4,)), dma((4,)),
        dma((SECTIONS, 8)), dma((SECTIONS, 8)),
        dma((SECTIONS, QPK + 1)), dma((SECTIONS, QPK + 1)),
        dma((SECTIONS, QPK + 1)), dma((SECTIONS, QPK + 1)),
        dma((SECTIONS, 4)), dma((SECTIONS, 4)), dma((SECTIONS, 4)), dma((SECTIONS, 4)),
    ]
    anywhere = pl.BlockSpec(memory_space=pl.ANY)
    whole = pl.BlockSpec(memory_space=pltpu.VMEM)
    return pl.pallas_call(
        fused_kernel,
        out_shape=jax.ShapeDtypeStruct(query_states.shape, BF16),
        in_specs=[
            anywhere, whole, anywhere, anywhere, whole, anywhere, anywhere,
            pl.BlockSpec(memory_space=pltpu.SMEM),
        ],
        out_specs=whole,
        scratch_shapes=scratch,
        compiler_params=pltpu.CompilerParams(
            collective_id=0, has_side_effects=True, vmem_limit_bytes=60 * 2**20
        ),
    )(
        hidden,
        kv_gain[None, :],
        kv_weight,
        query_states,
        query_gain,
        query_weight.reshape(SECTIONS, KVH, own, QPK * HD),
        output_weight.reshape(SECTIONS, KVH, own, QPK * HD),
        block_bounds,
    )


def choose(*args):
    tiles = lax.axis_size("row") // KVH
    if tiles == TILES and 2 * args[2].shape[0] % 128 == 0:
        return on_kernel(*args)
    return on_device(*args)


def solution(mesh):
    in_specs = (
        P(("groups", "row"), None),
        P(),
        P("row", None),
        P("row", "groups"),
        P(),
        P(None, "row", None, None),
        P(None, "row", None, None),
        P("groups", None),
    )
    out_specs = P("row", "groups")
    return jax.shard_map(
        choose, mesh=mesh, in_specs=in_specs, out_specs=out_specs, check_vma=False
    )
```

```python
import functools

import jax
import jax.numpy as jnp
from jax import lax
from jax.experimental import pallas as pl
from jax.experimental.pallas import tpu as pltpu
from jax.sharding import PartitionSpec as P

D = 5120
KVH = 8
HD = 128
QPK = 5
QBLK = 64
NQB = 2
SECTIONS = 2


CAP = 30.0
EPSILON = 1e-05


def swapped(value, axis, distance):
    mask = 2**distance
    pairs = [(source, source ^ mask) for source in range(lax.axis_size(axis))]
    return lax.ppermute(value, axis, pairs)


def halve_sum(first, second, bit_list, split_axis):
    device_index = lax.axis_index("row")
    for bit_number in reversed(bit_list):
        upper_half = device_index // 2**bit_number % 2
        first_low, first_high = jnp.split(first, 2, axis=split_axis)
        second_low, second_high = jnp.split(second, 2, axis=split_axis)
        kept_first = jnp.where(upper_half == 1, first_high, first_low)
        kept_second = jnp.where(upper_half == 1, second_high, second_low)
        sent_first = jnp.where(upper_half == 1, first_low, first_high)
        sent_second = jnp.where(upper_half == 1, second_low, second_high)
        got_first, got_second = (
            swapped(sent_first.astype(jnp.bfloat16), "row", bit_number).astype(sent_first.dtype),
            swapped(sent_second.astype(jnp.bfloat16), "row", bit_number).astype(sent_second.dtype),
        )
        first = kept_first + got_first
        second = kept_second + got_second
    return (first, second)


def halve_one(member, bit_list, split_axis):
    device_index = lax.axis_index("row")
    for bit_number in reversed(bit_list):
        upper_half = device_index // 2**bit_number % 2
        lower_piece, upper_piece = jnp.split(member, 2, axis=split_axis)
        kept = jnp.where(upper_half == 1, upper_piece, lower_piece)
        sent = jnp.where(upper_half == 1, lower_piece, upper_piece)
        member = kept + swapped(sent.astype(jnp.bfloat16), "row", bit_number).astype(sent.dtype)
    return member


def double_gather(gathered, bit_list, join_axis):
    device_index = lax.axis_index("row")
    for bit_number in bit_list:
        upper_half = device_index // 2**bit_number % 2
        partner = swapped(gathered, "row", bit_number)
        gathered = jnp.where(
            upper_half == 1,
            jnp.concatenate([partner, gathered], join_axis),
            jnp.concatenate([gathered, partner], join_axis),
        )
    return gathered


def attend_rows(queries, query_pos, query_floor, key_values, key_pos):
    row_count = queries.shape[0]
    head_width = key_values.shape[1] // 2
    head_count = queries.shape[1] // head_width
    key_part = key_values[:, :head_width]
    value_part = key_values[:, head_width:]
    grouped = queries.reshape(row_count, head_count, head_width)
    scores = jnp.einsum(
        "rhd,kd->rhk", grouped, key_part, preferred_element_type=jnp.float32
    ) * head_width ** (-0.5)
    capped = CAP * jnp.tanh(scores / CAP)
    visible = (key_pos[None, :] <= query_pos[:, None]) & (key_pos[None, :] >= query_floor[:, None])
    weights = jnp.where(visible[:, None, :], jnp.exp(capped), 0.0)
    totals = jnp.sum(weights, axis=2)
    weighted = jnp.einsum(
        "rhk,kd->rhd", weights.astype(jnp.bfloat16), value_part, preferred_element_type=jnp.float32
    )
    return (weighted.reshape(row_count, head_count * head_width), totals)


def on_device(
    hidden, kv_gain, kv_weight, query_states, query_gain, query_weight, output_weight, block_bounds
):
    lane_count = lax.axis_size("row")
    head_bits = KVH.bit_length() - 1
    total_bits = lane_count.bit_length() - 1
    tile_bits = list(range(head_bits))
    group_bits = list(range(head_bits, total_bits))
    tile_count = lane_count // KVH
    device_index = lax.axis_index("row")
    tile_index = device_index // KVH
    token_rows = hidden.shape[0]
    sub_rows = token_rows // tile_count
    pair_width = 2 * HD
    hidden_float = hidden.astype(jnp.float32)
    inverse = lax.rsqrt(jnp.mean(hidden_float * hidden_float, axis=1, keepdims=True) + EPSILON)
    normed = (hidden_float * inverse * kv_gain[None, :]).astype(jnp.bfloat16)
    grouped_rows = normed.reshape(tile_count, sub_rows, D)
    shard_rows = lax.all_gather(kv_weight, "row", axis=0, tiled=True)
    blocked = shard_rows.reshape(shard_rows.shape[0], KVH, pair_width)
    projected = jnp.einsum(
        "psd,dgc->pgsc", grouped_rows, blocked, preferred_element_type=jnp.float32
    )
    outgoing = projected.astype(jnp.bfloat16).reshape(lane_count, sub_rows, pair_width)
    arrived = lax.all_to_all(outgoing, "row", split_axis=0, concat_axis=0, tiled=True)
    key_values = arrived.reshape(lane_count * sub_rows, pair_width)
    source = jnp.arange(lane_count * sub_rows, dtype=jnp.int32)
    key_pos = source // sub_rows * token_rows + tile_index * sub_rows + source % sub_rows
    query_count = NQB * QBLK
    row_number = jnp.arange(query_count, dtype=jnp.int32)
    query_pos = (
        jnp.broadcast_to(block_bounds[:, 1:2], (NQB, QBLK)).reshape(query_count) + row_number % QBLK
    )
    query_floor = jnp.broadcast_to(block_bounds[:, 0:1], (NQB, QBLK)).reshape(query_count)
    rows_share = query_count // tile_count
    slice_depth = D // tile_count
    own_rows = query_states
    stream = double_gather(own_rows, tile_bits, 0)
    for section in range(SECTIONS):
        stream_float = stream.astype(jnp.float32)
        squares = jnp.sum(stream_float * stream_float, axis=0)
        gain_slice = lax.dynamic_slice_in_dim(
            query_gain[section], tile_index * slice_depth, slice_depth
        )
        scaled = (stream_float * gain_slice[:, None]).astype(jnp.bfloat16)
        partial_q = lax.dot_general(
            scaled,
            query_weight[section, 0],
            (((0,), (0,)), ((), ())),
            preferred_element_type=jnp.float32,
        )
        query_sum, square_sum = halve_sum(partial_q, squares, group_bits, 0)
        inverse_q = lax.rsqrt(square_sum / D + EPSILON)
        own_queries = (query_sum * inverse_q[:, None]).astype(jnp.bfloat16)
        all_queries = double_gather(own_queries, group_bits, 0)
        added_all, counted_all = attend_rows(
            all_queries, query_pos, query_floor, key_values, key_pos
        )
        accumulated, totals = halve_sum(added_all, counted_all, group_bits, 0)
        attended = (
            (accumulated.reshape(rows_share, QPK, HD) / totals[:, :, None])
            .reshape(rows_share, QPK * HD)
            .astype(jnp.bfloat16)
        )
        all_attended = double_gather(attended, group_bits, 0)
        update = lax.dot_general(
            output_weight[section, 0],
            all_attended,
            (((1,), (1,)), ((), ())),
            preferred_element_type=jnp.float32,
        )
        own_update = halve_one(update, tile_bits, 0)
        own_rows = (own_rows.astype(jnp.float32) + own_update).astype(jnp.bfloat16)
        if section + 1 < SECTIONS:
            stream = double_gather(own_rows, tile_bits, 0)
    return own_rows


MESH = pl.DeviceIdType.MESH
TILES = 2
CHIPS = KVH // 2
ORDER = (3, 1, 2, 0)
PAIR = 2 * HD
F32 = jnp.float32
BF16 = jnp.bfloat16


def fused_kernel(
    hidden, kv_gain, kv_weight, query_states, query_gain, query_weight, output_weight, bounds,
    out,
    hid, nrm, kvw, xg, wkv, acc, sbuf, rbuf, kvs,
    wq, wo, st, gcol, qsend, qrecv, qh, sqs, sqr,
    oacc, osend, orecv, totb, tsend, trecv, att, us1, ur1, us2, ur2, upd,
    lsem, lw, lx, sx, rx, sf, sw, sy, rw, sk, rk, sst, rst, sq_s, sq_r, so_s, so_r, s1, r1, s2, r2,
):
    tokens, features = hidden.shape
    own = kv_weight.shape[0]
    depth = features // TILES
    chip_rows = 2 * own
    keys = KVH * tokens
    me = lax.axis_index("row")
    plane = lax.axis_index("groups")
    tile = me // KVH
    group = me % KVH
    place = group // 2
    core = group % 2
    upper, side = place // 2, place % 2
    other, partner = 1 - tile, 1 - core

    def chip(k):
        a, b = k // 2, k % 2
        return 2 * (upper + a - 2 * a * upper) + (side + b - 2 * b * side)

    def device(in_tile, q, in_core):
        return in_tile * KVH + 2 * q + in_core

    pair = device(tile, place, partner)
    mirror = device(other, place, core)
    mirror_pair = device(other, place, partner)
    pending = []

    def send(src, dst, send_sem, recv_sem, target):
        copy = pltpu.make_async_remote_copy(
            src_ref=src, dst_ref=dst, send_sem=send_sem, recv_sem=recv_sem,
            device_id=target if isinstance(target, dict) else {"row": target},
            device_id_type=MESH,
        )
        copy.start()
        pending.append(copy)

    def arrived(dst, send_sem, recv_sem):
        pltpu.make_async_remote_copy(
            src_ref=dst, dst_ref=dst, send_sem=send_sem, recv_sem=recv_sem,
            device_id={"row": pair}, device_id_type=MESH,
        ).wait_recv()

    load_states = pltpu.make_async_copy(query_states, st.at[0, group], lsem.at[0])
    load_kvw = pltpu.make_async_copy(kv_weight, kvw, lsem.at[1])
    load_hidden = pltpu.make_async_copy(hidden, hid, lsem.at[2])
    load_wq = pltpu.make_async_copy(query_weight, wq, lsem.at[3])
    load_wo = pltpu.make_async_copy(output_weight, wo, lsem.at[4])
    for load in (load_states, load_kvw, load_hidden, load_wq, load_wo):
        load.start()

    barrier = pltpu.get_barrier_semaphore()
    peers = [device(tile, chip(k), cc) for k in (1, 2, 3) for cc in (core, partner)]
    peers += [pair, mirror, mirror_pair]
    for peer in peers:
        pl.semaphore_signal(barrier, inc=1, device_id={"row": peer}, device_id_type=MESH)
    across = {"groups": 1 - plane}
    pl.semaphore_signal(barrier, inc=1, device_id=across, device_id_type=MESH)
    pl.semaphore_wait(barrier, len(peers) + 1)

    def stream_sends(s):
        for k in ORDER:
            target = pair if k == 0 else device(tile, chip(k), core)
            send(st.at[s, group], st.at[s, group], sst.at[s, k], rst.at[s, group], target)

    def stream_relay(s):
        for k in (1, 2, 3):
            source = 2 * chip(k) + core
            arrived(st.at[s, source], sst.at[s, k], rst.at[s, source])
            send(st.at[s, source], st.at[s, source], sst.at[s, 4 + k], rst.at[s, source], pair)
        for k in range(CHIPS):
            source = 2 * chip(k) + partner
            arrived(st.at[s, source], sst.at[s, k], rst.at[s, source])

    load_states.wait()
    stream_sends(0)

    load_kvw.wait()
    local = []

    def head_columns(k, in_core):
        return kvw.at[:, pl.ds(pl.multiple_of((2 * chip(k) + in_core) * PAIR, PAIR), PAIR)]

    def mirror_sends(i):
        k = CHIPS - 1 - i - 2 * plane
        send(head_columns(k, core), wkv.at[1, k, core], sw.at[0, i], rw.at[1, k, core], mirror)
        send(head_columns(k, partner), wkv.at[1, k, core], sw.at[1, i], rw.at[1, k, core], mirror_pair)

    def mirror_relay(i):
        k = CHIPS - 1 - i - 2 * plane
        for cc in (0, 1):
            arrived(wkv.at[1, k, cc], sw.at[0, i], rw.at[1, k, cc])
            send(wkv.at[1, k, cc], wkv.at[1, k, cc], sy.at[i, cc], rw.at[1, k, cc], across)

    def mirror_take(i):
        k = CHIPS - 1 - i - 2 * (1 - plane)
        for cc in (0, 1):
            arrived(wkv.at[1, k, cc], sw.at[0, i], rw.at[1, k, cc])

    mirror_sends(0)
    for k in ORDER:
        send(head_columns(k, partner), wkv.at[0, k, core], sw.at[2, k], rw.at[0, k, core], pair)
        copy = pltpu.make_async_copy(head_columns(k, core), wkv.at[0, k, core], lw.at[k])
        copy.start()
        local.append(copy)

    load_hidden.wait()
    step_rows = 32

    def normalise(i, carry):
        rows = pl.ds(pl.multiple_of(i * step_rows, step_rows), step_rows)
        value = hid[rows, :].astype(F32)
        inverse = lax.rsqrt(jnp.mean(value * value, axis=1, keepdims=True) + EPSILON)
        nrm[rows, :] = (value * inverse * kv_gain[...]).astype(BF16)
        return carry

    lax.fori_loop(0, tokens // step_rows, normalise, 0)

    def feature_block(r, q):
        start = (tile if r == 0 else other) * depth + q * chip_rows
        return nrm.at[:, pl.ds(pl.multiple_of(start, 128), chip_rows)]

    for r in (0, 1):
        for k in ORDER:
            target = pair if k == 0 else device(tile, chip(k), core)
            send(feature_block(r, chip(k)), xg.at[r, group], sx.at[r, k], rx.at[r, group], target)
        copy = pltpu.make_async_copy(feature_block(r, place), xg.at[r, group], lx.at[r])
        copy.start()
        local.append(copy)
    mirror_sends(1)

    for s in range(SECTIONS):
        def turn(i, carry, s=s):
            cols = pl.ds(pl.multiple_of(tile * depth + i * 128, 128), 128)
            row = query_gain[s : s + 1, cols]
            gcol[s, pl.ds(pl.multiple_of(i * 128, 128), 128), :] = jnp.broadcast_to(row, (128, 128)).T
            return carry

        lax.fori_loop(0, depth // 128, turn, 0)

    def query_partial(s):
        total = jnp.zeros((NQB * QBLK, QPK * HD), F32)
        squares = jnp.zeros((1, NQB * QBLK), F32)
        for j in range(KVH):
            value = st[s, j].astype(F32)
            squares = squares + jnp.sum(value * value, axis=0, keepdims=True)
            scaled = (value * gcol[s, j * own : (j + 1) * own, :]).astype(BF16)
            total = total + lax.dot_general(
                scaled, wq[s, j], (((0,), (0,)), ((), ())), preferred_element_type=F32
            )
        for h in range(QPK):
            part = total[:, h * HD : (h + 1) * HD]
            qh[h] = part
            qsend[s, h] = part.astype(BF16)
            if h == 0:
                sqs[s] = jnp.broadcast_to(squares, sqs.shape[1:])
                send(sqs.at[s], sqr.at[s], sq_s.at[s, QPK], sq_r.at[s, QPK], mirror)
            send(qsend.at[s, h], qrecv.at[s, h], sq_s.at[s, h], sq_r.at[s, h], mirror)

    def query_finish(s):
        arrived(sqr.at[s], sq_s.at[s, QPK], sq_r.at[s, QPK])
        squares = sqs[s] + sqr[s]
        inverse = lax.rsqrt(squares[0:1, :] / features + EPSILON)
        return jnp.broadcast_to(inverse, (NQB * QBLK, NQB * QBLK)).T

    qfin = osend.at[SECTIONS]

    stream_relay(0)
    load_wq.wait()
    query_partial(0)
    mirror_relay(0)

    for r in (0, 1):
        for k in (1, 2, 3):
            source = 2 * chip(k) + core
            arrived(xg.at[r, source], sx.at[r, k], rx.at[r, source])
            send(xg.at[r, source], xg.at[r, source], sf.at[r, k], rx.at[r, source], pair)

    row_step = 256
    sources = row_step // tokens

    def product(r, k, i):
        left = xg[r, pl.ds(i * sources, sources)].reshape(row_step, chip_rows)
        right = wkv[r, k].reshape(chip_rows, PAIR)
        return jnp.dot(left, right, preferred_element_type=F32)

    def take(r):
        for k in range(CHIPS):
            source = 2 * chip(k) + partner
            arrived(xg.at[r, source], sx.at[r, k], rx.at[r, source])

    for copy in local:
        copy.wait()
    take(0)
    for k in ORDER:
        arrived(wkv.at[0, k, partner], sw.at[2, k], rw.at[0, k, partner])

        def first(i, carry, k=k):
            acc[k, pl.ds(pl.multiple_of(i * row_step, row_step), row_step), :] = product(0, k, i)
            return carry

        lax.fori_loop(0, keys // row_step, first, 0)
    take(1)
    for k in ORDER:
        if k == CHIPS - 1:
            mirror_take(0)
        if k == 1:
            mirror_relay(1)
        if k == 2:
            mirror_take(1)
            arrived(rbuf.at[3], sk.at[3], rk.at[3])

        def second(i, carry, k=k):
            rows = pl.ds(pl.multiple_of(i * row_step, row_step), row_step)
            value = acc[k, rows, :] + product(1, k, i)
            if k == 2:
                value = value + rbuf[3, rows, :].astype(F32)
            if k == 0:
                acc[k, rows, :] = value
            else:
                sbuf[k, rows, :] = value.astype(BF16)
            return carry

        lax.fori_loop(0, keys // row_step, second, 0)
        if k:
            send(sbuf.at[k], rbuf.at[k], sk.at[k], rk.at[k], device(tile, chip(1 if k == 3 else k), core))
    for k in (1, 2):
        arrived(rbuf.at[k], sk.at[k], rk.at[k])

    def join(i, carry):
        rows = pl.ds(pl.multiple_of(i * row_step, row_step), row_step)
        value = acc[0, rows, :]
        for k in (1, 2):
            value = value + rbuf[k, rows, :].astype(F32)
        kvs[rows, :] = value.astype(BF16)
        return carry

    lax.fori_loop(0, keys // row_step, join, 0)

    load_wo.wait()
    rows_of = NQB * QBLK
    for s in range(SECTIONS):
        column = query_finish(s)

        def attend(b, carry, h):
            rows = pl.ds(pl.multiple_of(b * QBLK, QBLK), QBLK)
            score = lax.dot_general(
                qfin[h, rows, :], kvs[:, :HD], (((1,), (1,)), ((), ())), preferred_element_type=F32
            ) * HD ** (-0.5)
            capped = CAP * jnp.tanh(score / CAP)
            position = tile * keys + lax.broadcasted_iota(jnp.int32, (QBLK, keys), 1)
            last = bounds[b, 1] + lax.broadcasted_iota(jnp.int32, (QBLK, keys), 0)
            visible = (position <= last) & (position >= bounds[b, 0])
            weight = jnp.where(visible, jnp.exp(capped), 0.0)
            totb[h, rows, :] = jnp.broadcast_to(jnp.sum(weight, axis=1, keepdims=True), (QBLK, HD))
            oacc[h, rows, :] = jnp.dot(weight.astype(BF16), kvs[:, HD:], preferred_element_type=F32)
            return carry

        for h in range(QPK):
            arrived(qrecv.at[s, h], sq_s.at[s, h], sq_r.at[s, h])
            qfin[h] = ((qh[h] + qrecv[s, h].astype(F32)) * column).astype(BF16)
            lax.fori_loop(0, NQB, functools.partial(attend, h=h), 0)
            osend[s, h] = oacc[h].astype(BF16)
            send(osend.at[s, h], orecv.at[s, h], so_s.at[s, h], so_r.at[s, h], mirror)
        lane = lax.broadcasted_iota(jnp.int32, (rows_of, HD), 1)
        table = jnp.zeros((rows_of, HD), F32)
        for h in range(QPK):
            table = jnp.where(lane == h, totb[h], table)
        tsend[s] = table.T[0:8, :]
        send(tsend.at[s], trecv.at[s], so_s.at[s, QPK], so_r.at[s, QPK], mirror)
        arrived(trecv.at[s], so_s.at[s, QPK], so_r.at[s, QPK])
        table = jnp.concatenate([trecv[s], jnp.zeros((HD - 8, rows_of), F32)], axis=0).T
        for h in range(QPK):
            arrived(orecv.at[s, h], so_s.at[s, h], so_r.at[s, h])
            total = totb[h] + table[:, h : h + 1]
            value = (oacc[h] + orecv[s, h].astype(F32)) / total
            att[:, h * HD : (h + 1) * HD] = value.astype(BF16)

        def update(j):
            return lax.dot_general(
                wo[s, j], att[...], (((1,), (1,)), ((), ())), preferred_element_type=F32
            )

        for k in ORDER:
            us1[s, k] = update(2 * chip(k) + partner).astype(BF16)
            send(us1.at[s, k], ur1.at[s, k], s1.at[s, k], r1.at[s, k], pair)
        for k in ORDER:
            value = update(2 * chip(k) + core)
            arrived(ur1.at[s, k], s1.at[s, k], r1.at[s, k])
            value = value + ur1[s, k].astype(F32)
            if k:
                us2[s, k] = value.astype(BF16)
                send(us2.at[s, k], ur2.at[s, k], s2.at[s, k], r2.at[s, k], device(tile, chip(k), core))
            else:
                upd[...] = value + st[s, group].astype(F32)
        for k in (1, 2, 3):
            arrived(ur2.at[s, k], s2.at[s, k], r2.at[s, k])
        value = upd[...]
        for k in (1, 2, 3):
            value = value + ur2[s, k].astype(F32)
        if s + 1 < SECTIONS:
            st[s + 1, group] = value.astype(BF16)
            stream_sends(s + 1)
            stream_relay(s + 1)
            query_partial(s + 1)
        else:
            out[...] = value.astype(BF16)
    for copy in pending:
        copy.wait_send()


def on_kernel(
    hidden, kv_gain, kv_weight, query_states, query_gain, query_weight, output_weight, block_bounds
):
    tokens, features = hidden.shape
    own = kv_weight.shape[0]
    depth = features // TILES
    chip_rows = 2 * own
    keys = KVH * tokens
    rows = NQB * QBLK
    vmem, dma = pltpu.VMEM, pltpu.SemaphoreType.DMA
    scratch = [
        vmem((tokens, features), BF16),
        vmem((tokens, features), BF16),
        vmem(kv_weight.shape, BF16),
        vmem((TILES, KVH, tokens, chip_rows), BF16),
        vmem((TILES, CHIPS, 2, own, PAIR), BF16),
        vmem((CHIPS, keys, PAIR), F32),
        vmem((CHIPS, keys, PAIR), BF16),
        vmem((CHIPS, keys, PAIR), BF16),
        vmem((keys, PAIR), BF16),
        vmem((SECTIONS, KVH, own, QPK * HD), BF16),
        vmem((SECTIONS, KVH, own, QPK * HD), BF16),
        vmem((SECTIONS, KVH, own, rows), BF16),
        vmem((SECTIONS, depth, rows), F32),
        vmem((SECTIONS, QPK, rows, HD), BF16),
        vmem((SECTIONS, QPK, rows, HD), BF16),
        vmem((QPK, rows, HD), F32),
        vmem((SECTIONS, 8, rows), F32),
        vmem((SECTIONS, 8, rows), F32),
        vmem((QPK, rows, HD), F32),
        vmem((SECTIONS + 1, QPK, rows, HD), BF16),
        vmem((SECTIONS, QPK, rows, HD), BF16),
        vmem((QPK, rows, HD), F32),
        vmem((SECTIONS, 8, rows), F32),
        vmem((SECTIONS, 8, rows), F32),
        vmem((rows, QPK * HD), BF16),
        vmem((SECTIONS, CHIPS, own, rows), BF16),
        vmem((SECTIONS, CHIPS, own, rows), BF16),
        vmem((SECTIONS, CHIPS, own, rows), BF16),
        vmem((SECTIONS, CHIPS, own, rows), BF16),
        vmem((own, rows), F32),
        dma((5,)), dma((4,)), dma((2,)), dma((2, 4)), dma((2, 8)), dma((2, 4)),
        dma((3, 4)), dma((2, 2)), dma((2, 4, 2)), dma((4,)), dma((4,)),
        dma((SECTIONS, 8)), dma((SECTIONS, 8)),
        dma((SECTIONS, QPK + 1)), dma((SECTIONS, QPK + 1)),
        dma((SECTIONS, QPK + 1)), dma((SECTIONS, QPK + 1)),
        dma((SECTIONS, 4)), dma((SECTIONS, 4)), dma((SECTIONS, 4)), dma((SECTIONS, 4)),
    ]
    anywhere = pl.BlockSpec(memory_space=pl.ANY)
    whole = pl.BlockSpec(memory_space=pltpu.VMEM)
    return pl.pallas_call(
        fused_kernel,
        out_shape=jax.ShapeDtypeStruct(query_states.shape, BF16),
        in_specs=[
            anywhere, whole, anywhere, anywhere, whole, anywhere, anywhere,
            pl.BlockSpec(memory_space=pltpu.SMEM),
        ],
        out_specs=whole,
        scratch_shapes=scratch,
        compiler_params=pltpu.CompilerParams(
            collective_id=0, has_side_effects=True, vmem_limit_bytes=60 * 2**20
        ),
    )(
        hidden,
        kv_gain[None, :],
        kv_weight,
        query_states,
        query_gain,
        query_weight.reshape(SECTIONS, KVH, own, QPK * HD),
        output_weight.reshape(SECTIONS, KVH, own, QPK * HD),
        block_bounds,
    )


def choose(*args):
    tiles = lax.axis_size("row") // KVH
    if tiles == TILES and 2 * args[2].shape[0] % 128 == 0:
        return on_kernel(*args)
    return on_device(*args)


def solution(mesh):
    in_specs = (
        P(("groups", "row"), None),
        P(),
        P("row", None),
        P("row", "groups"),
        P(),
        P(None, "row", None, None),
        P(None, "row", None, None),
        P("groups", None),
    )
    out_specs = P("row", "groups")
    return jax.shard_map(
        choose, mesh=mesh, in_specs=in_specs, out_specs=out_specs, check_vma=False
    )
```
